1024 devices in a mesh: group: 4 (over z_lo), seq: 32 (over z_hi, y), shard: 8 (over x, core).
Axes of the slice: x: 4, y: 8, z: 16 (z_hi: 4, z_lo: 4; z = z_hi * 4 + z_lo), core: 2. Of those that a mesh axis runs over, the one named last changes fastest.
Arguments:
- text_rows: bfloat16 [32768, 8, 1280], P(('group', 'seq'), 'shard'), may hold values from -64 to 64
- vis_rows: bfloat16 [8192, 8, 1280], P(('group', 'seq', 'shard')), may hold values from -6 to 6
- vis_dest: int32 [8192, 1], P(('group', 'seq', 'shard')), may hold values from 0 to 31; in each aligned block of 64 rows (0 to 63, 64 to 127, ...) at most 4 rows name the same one
- segments: int32 [49152], P(('group', 'seq')), may hold values from 0 to 63, never falling along the last dimension, each value on 1 to 1536 neighbouring positions
Outputs:
- attended: bfloat16 [49152, 8, 1024], P(('group', 'seq'), 'shard')
The draws below stay inside these ranges and needn't reach their ends.
Inputs may be any that keep to these rules, and one draw needn't show every extreme that they name: `vis_dest`: in each aligned block of 64 rows (the visual rows listed by one index of group and seq, in device order), no value is named by more than 4 rows, and this bound is reached. `segments`: ids never fall along the sequence; each document covers 1 to 1536 positions, and one covers exactly 1536.
All inputs are finite; a program needn't handle non-finite values.
Results may differ from the reference program's by a relative error of at most 0.0028.
Values may be sent and summed in bfloat16 or wider, within the bound.
No kernel may reach another device: no remote copies, remote signals or barrier semaphores. Data moves between devices by JAX's collectives and lax.ppermute only.
A program may use at most 32 MiB of HBM per device.

```python
import math
import jax
import jax.numpy as jnp
import numpy as np
from jax import lax

KVH = 8
GQ = 8
DH = 128
TEXT_DEV = 256
CAP = 4
REACH = 4
ROWS = 384
SLOTS = 49152
TEXT_ALL = 32768
VIS_DEV = 8
VIS_ALL = 8192
DOCMAX = 1536
DOCS = 64
N_GROUP = 4
N_SEQ = 32
N_SHARD = 8


def draw_text_rows(key, part):
    row_width = (GQ + 2) * DH
    drawn = jax.random.normal(key, (TEXT_ALL, KVH, row_width), jnp.float32)
    spread = jnp.concatenate([jnp.full((GQ * DH,), 2.5, jnp.float32), jnp.ones((2 * DH,), jnp.float32)])
    result_rows = drawn * spread
    return result_rows.astype(jnp.bfloat16)


def level_of(rng, extent, shards, least, largest):
    level, own = 1.0, jax.random.fold_in(rng, 6)
    for position, parts in shards:
        draws = jnp.exp(jax.random.uniform(jax.random.fold_in(own, position), (parts,), jnp.float32, least / len(shards), largest / len(shards)))
        level = level * jnp.repeat(draws, extent[position] // parts).reshape([-1 if axis == position else 1 for axis in range(len(extent))])
    return level


def profile(number_of, total, reach, slope):
    loads = [(1 << 20) // math.isqrt(rank ** slope) + 1 for rank in range(2, number_of + 1)]
    surplus, counts = total - reach - (number_of - 1), [1] * (number_of - 1)
    while surplus > 0:
        movable = [i for i in range(number_of - 1) if counts[i] < reach]
        whole, remaining = sum([loads[i] for i in movable]), surplus
        for i in movable:
            addition = min(reach - counts[i], max(1, remaining * loads[i] // whole), surplus)
            counts[i] = counts[i] + addition
            surplus = surplus - addition
    return np.array([reach] + counts)


def uneven(stream_key, number_of, total, bound, lean):
    if number_of == 2:
        one = jax.random.randint(stream_key, (), max(1, total - bound), min(bound, total - 1) + 1)
        return jnp.stack([one, total - one])
    lengths = jnp.asarray(profile(number_of, total, bound, lean), jnp.int32)
    pairs = (number_of - 1) // 2
    source_of, taker = lengths[1:1 + 2 * pairs:2], lengths[2:2 + 2 * pairs:2]
    room = jnp.minimum(source_of - 1, bound - taker)
    shifted = jax.random.randint(jax.random.fold_in(stream_key, 1), (pairs,), 0, 1 << 20) % (room + 1)
    lengths = lengths.at[1:1 + 2 * pairs:2].set(source_of - shifted).at[2:2 + 2 * pairs:2].set(taker + shifted)
    return lengths[jax.random.permutation(jax.random.fold_in(stream_key, 2), number_of)]


def assign_block(stream_key, own, number, rows, number_of, top, limit, skew):
    sequence = jax.random.permutation(stream_key, number_of)
    heavy_load, usual = load_shares(number_of, rows * top, limit, skew, True), load_shares(number_of, rows * top, limit, skew, False)
    places = jnp.arange(number_of)

    def named(lengths, turn):
        used = int((lengths > 0).sum())
        fixed = max(1, used // 4)
        passed = fixed + (places - fixed + turn * (used - fixed)) % max(1, number_of - fixed)
        return jnp.zeros((number_of,), jnp.int32).at[sequence[jnp.where(places < fixed, places, passed)]].set(jnp.asarray(lengths, jnp.int32))

    lengths = jnp.where(number % 4 == 0, named(heavy_load, number // 4), named(usual, number - number // 4 - 1))
    mixed = jax.random.permutation(jax.random.fold_in(own, 3), number_of)
    giver, receiver = mixed[0:number_of // 2 * 2:2], mixed[1:number_of // 2 * 2:2]
    room = jnp.minimum(lengths[giver] - 1, limit - lengths[receiver]) // 2
    room = jnp.where((giver == sequence[0]) | (receiver == sequence[0]) | (lengths[receiver] == 0), 0, jnp.maximum(room, 0))
    passed = jax.random.randint(jax.random.fold_in(own, 4), (number_of // 2,), 0, 1 << 20) % (room + 1)
    lengths = lengths.at[giver].add(-passed).at[receiver].add(passed)
    members = jnp.searchsorted(jnp.cumsum(lengths), jnp.arange(rows * top), side="right").astype(jnp.int32)
    listing = members.reshape(top, rows).T
    listing = listing[jax.random.permutation(jax.random.fold_in(own, 1), rows)]
    turn = jax.random.randint(jax.random.fold_in(own, 2), (rows, 1), 0, top)
    return jnp.take_along_axis(listing, (jnp.arange(top)[None, :] + turn) % top, axis=1)


def load_shares(count, total, limit, lean, full):
    loads = [(1 << 20) // math.isqrt(grade ** lean) + 1 for grade in range(1, count + 1)]
    largest = limit if full else min(limit, max(-(-total // count), total * loads[0] // sum(loads)))
    least = 1 if total - largest >= count - 1 else 0
    given, spare = [largest] + [least] * (count - 1), total - largest - least * (count - 1)
    while spare > 0:
        free = [i for i in range(1, count) if given[i] < largest] or [i for i in range(1, count) if given[i] < limit]
        whole, remaining = sum([loads[i] for i in free]), spare
        for i in free:
            extra = min(limit - given[i], max(1, remaining * loads[i] // whole), spare)
            given[i] = given[i] + extra
            spare = spare - extra
    return np.array(given)


def normal_values(own_key, extent, scale, most, split=(), kind=jnp.bfloat16):
    gain = level_of(own_key, extent, split, -0.22, 0.18) if split else 1.0
    values = jax.random.normal(own_key, extent, jnp.float32) * scale * gain
    return jnp.minimum(jnp.maximum(values, -most), most).astype(kind)


def setup_inputs(seed: int = 0) -> dict:
    key_of = jax.random.split(jax.random.key(seed), 5)
    text_rows = draw_text_rows(jax.random.fold_in(key_of[4], 71), 0)
    vis_rows = normal_values(key_of[1], (VIS_ALL, KVH, (GQ + 2) * DH), 1.0, 6.0, ((0, 1024),))
    vis_dest_keys = jax.random.split(jax.random.fold_in(key_of[2], 1), VIS_ALL // (N_SHARD * VIS_DEV))
    vis_dest_turns = jax.random.permutation(jax.random.fold_in(key_of[2], 3), VIS_ALL // (N_SHARD * VIS_DEV))
    vis_dest = jax.vmap(lambda own, number: assign_block(jax.random.fold_in(key_of[2], 2), own, number, N_SHARD * VIS_DEV, N_SEQ, 1, CAP, 2))(vis_dest_keys, vis_dest_turns).reshape((VIS_ALL, 1))
    segments = jnp.searchsorted(jnp.cumsum(uneven(key_of[3], DOCS, SLOTS, DOCMAX, 2)), jnp.arange(SLOTS), side="right").astype(jnp.int32)
    return dict(text_rows=text_rows, vis_rows=vis_rows, vis_dest=vis_dest, segments=segments)


def reference(text_rows, vis_rows, vis_dest, segments):
    blocks = N_GROUP * N_SEQ
    block_rows = N_SHARD * VIS_DEV
    slot_count = N_SEQ * CAP
    row_width = (GQ + 2) * DH
    target = vis_dest[:, 0].reshape(blocks, block_rows)
    onehot = (target[:, :, None] == jnp.arange(N_SEQ, dtype=jnp.int32)[None, None, :]).astype(jnp.int32)
    before = jnp.cumsum(onehot, axis=1) - onehot
    slot_rank = jnp.sum(before * onehot, axis=2)
    source = jnp.arange(blocks, dtype=jnp.int32)[:, None]
    owner_block = (source // N_SEQ) * N_SEQ + target
    flat_slot = ((owner_block * N_SEQ + source % N_SEQ) * CAP + slot_rank).reshape(-1).astype(jnp.int32)
    slot_rows = jnp.zeros((blocks * slot_count, KVH, row_width), vis_rows.dtype).at[flat_slot].set(vis_rows)
    filled = jnp.zeros((blocks * slot_count,), jnp.int32).at[flat_slot].set(1)
    seq_rows = jnp.concatenate([text_rows.reshape(blocks, TEXT_DEV, KVH, row_width), slot_rows.reshape(blocks, slot_count, KVH, row_width)], axis=1).reshape(blocks * ROWS, KVH, row_width)
    live_rows = jnp.concatenate([jnp.ones((blocks, TEXT_DEV), jnp.int32), filled.reshape(blocks, slot_count)], axis=1).reshape(-1)
    doc_tag = jnp.where(live_rows > 0, segments + 1, 0).astype(jnp.int32)
    margin = REACH * ROWS
    keyval = jnp.concatenate([jnp.zeros((margin, KVH, 2 * DH), seq_rows.dtype), seq_rows[:, :, GQ * DH:]], axis=0)
    tag_pad = jnp.concatenate([jnp.zeros((margin,), jnp.int32), doc_tag])
    key_place = jnp.arange((REACH + 1) * ROWS, dtype=jnp.int32) - margin
    row_place = jnp.arange(ROWS, dtype=jnp.int32)
    score_scale = DH ** -0.5

    def one_block(block_index):
        first_row = (block_index * ROWS).astype(jnp.int32)
        queries = lax.dynamic_slice_in_dim(seq_rows, first_row, ROWS, 0)[:, :, :GQ * DH]
        queries = queries.reshape(ROWS, KVH, GQ, DH).astype(jnp.float32)
        key_rows = lax.dynamic_slice_in_dim(keyval, first_row, (REACH + 1) * ROWS, 0).astype(jnp.float32)
        key_tags = lax.dynamic_slice_in_dim(tag_pad, first_row, (REACH + 1) * ROWS, 0)
        query_segs = lax.dynamic_slice_in_dim(segments, first_row, ROWS, 0)
        query_live = lax.dynamic_slice_in_dim(live_rows, first_row, ROWS, 0) > 0
        visible = (key_place[None, :] <= row_place[:, None]) & (key_tags[None, :] == (query_segs + 1)[:, None]) & query_live[:, None]
        scores = jnp.einsum("rgqd,kgd->gqrk", queries, key_rows[:, :, :DH]) * score_scale
        scores = jnp.where(visible[None, None], scores, -1e30)
        row_max = jnp.max(scores, axis=3, keepdims=True)
        weights = jnp.where(visible[None, None], jnp.exp(scores - row_max), 0.0)
        row_total = jnp.where(query_live[None, None, :], jnp.sum(weights, axis=3), 1.0)
        rounded = lax.optimization_barrier(weights.astype(jnp.bfloat16)).astype(jnp.float32)
        weighted = jnp.einsum("gqrk,kgd->gqrd", rounded, key_rows[:, :, DH:])
        result = (weighted / row_total[..., None]).astype(jnp.bfloat16)
        return result.transpose(2, 0, 1, 3).reshape(ROWS, KVH, GQ * DH)

    outputs = lax.map(one_block, jnp.arange(blocks, dtype=jnp.int32))
    return outputs.reshape(blocks * ROWS, KVH, GQ * DH)
```

```python
import functools

import jax
import jax.numpy as jnp
from jax import lax
from jax.experimental import pallas as pl
from jax.experimental.pallas import tpu as pltpu
from jax.sharding import PartitionSpec as P

GQ = 8
DH = 128
CAP = 4
REACH = 4
RING = 8
LANES = 128
DEAD = 64.0
BIG = 1e30
SCALE = DH ** (-0.5) * 1.4426950408889634
F32 = jnp.float32
BF16 = jnp.bfloat16


def iota(shape, dim):
    return lax.broadcasted_iota(jnp.int32, shape, dim)


def dot(a, b):
    return jnp.dot(a, b, preferred_element_type=F32)


def dot_nt(a, b):
    return lax.dot_general(a, b, (((1,), (1,)), ((), ())), preferred_element_type=F32)


def ones_where(cond):
    return jnp.where(cond, 1.0, 0.0)


def prep_kernel(per_dev, heads, rows_ref, dest_ref, out_ref):
    count = per_dev * heads
    wide = rows_ref.shape[1]
    a, b = iota((count, count), 0), iota((count, count), 1)
    move = ones_where(b == (a % per_dev) * heads + a // per_dev).astype(BF16)
    out_ref[:, :wide] = dot(move, rows_ref[...]).astype(BF16)
    pick = ones_where(iota((count, per_dev), 1) == iota((count, per_dev), 0) % per_dev).astype(BF16)
    dest = jnp.broadcast_to(dest_ref[...].astype(F32).astype(BF16), (per_dev, LANES))
    out_ref[:, wide:] = dot(pick, dest).astype(BF16)


def slot_row(own_ref):
    count = own_ref.shape[0]
    wide = own_ref.shape[1] - LANES
    named = own_ref[:, wide:].astype(F32).astype(jnp.int32)
    onehot = ones_where(named == iota((count, LANES), 1)).astype(BF16)
    same = dot_nt(onehot, onehot)
    a, b = iota((count, count), 0), iota((count, count), 1)
    rank = jnp.sum(jnp.where(a < b, same, 0.0), axis=0, keepdims=True)
    dest = dot_nt(iota((8, LANES), 1).astype(F32).astype(BF16), onehot)[0:1]
    return dest * CAP + rank


def place(ids, slots):
    return ones_where(ids.astype(F32) == slots)


def tail_kernel(first, own_ref, tail_ref):
    count = own_ref.shape[0]
    q = GQ * DH
    slots = slot_row(own_ref)
    put = place(iota((REACH * CAP, count), 0) + first, slots)
    got = dot(put.astype(BF16), own_ref[:, q : q + 2 * DH])
    filled = jnp.sum(put, axis=1, keepdims=True)
    tail_ref[...] = jnp.where(filled > 0, got, DEAD).astype(BF16)


def pack_kernel(own_ref, tail_ref, out_ref):
    count = own_ref.shape[0]
    rows = out_ref.shape[0]
    q = GQ * DH
    slots = slot_row(own_ref)
    r = iota((rows, count), 0)
    sid = (r // 8) * CAP + r % CAP
    low = (r % 8) < CAP
    put0 = place(jnp.where(low, sid, -1000), slots)
    put1 = place(jnp.where(low, -1000, sid), slots)
    put0_b = put0.astype(BF16)
    base = dot(put0_b, own_ref[:, : q + DH])
    fill0 = jnp.sum(put0, axis=1, keepdims=True)
    first = base[:, :DH] + dot(put1.astype(BF16), own_ref[:, q + DH : q + 2 * DH])
    fill = fill0 + jnp.sum(put1, axis=1, keepdims=True)
    out_ref[:, :DH] = jnp.where(fill > 0, first, DEAD).astype(BF16)
    rt = iota((rows, REACH * CAP), 0)
    sid_t = (rt // 8) * CAP + rt % CAP
    low_t = (rt % 8) < CAP
    j = iota((rows, REACH * CAP), 1)
    for k in range(1, REACH + 1):
        put = place(jnp.where(low, -1000, sid - CAP * k), slots)
        old = ones_where(jnp.where(low_t, -1000, sid_t - CAP * k + REACH * CAP) == j)
        lo = DH + 2 * DH * (k - 1)
        val = (
            base[:, lo : lo + 2 * DH]
            + dot(put.astype(BF16), own_ref[:, q : q + 2 * DH])
            + dot(old.astype(BF16), tail_ref[...])
        )
        fill = fill0 + jnp.sum(put, axis=1, keepdims=True) + jnp.sum(old, axis=1, keepdims=True)
        out_ref[:, lo : lo + 2 * DH] = jnp.where(fill > 0, val, DEAD).astype(BF16)


def attend_kernel(text_ref, seg_ref, came_ref, h1, h2, h3, h4, out_ref, qv, kk, kx, vv, qx, own_bias, ss):
    halos = (h1, h2, h3, h4)
    text = text_ref.shape[0]
    vis = came_ref.shape[0] // 2
    rows = text + vis
    q = GQ * DH
    a, b = iota((vis, 2 * vis), 0), iota((vis, 2 * vis), 1)
    src = (a // CAP) * 8 + a % CAP
    low = dot(ones_where(b == src).astype(BF16), came_ref[...])
    high = dot(ones_where(b == src + CAP).astype(BF16), came_ref[...])
    qv[...] = low[:, :q].astype(BF16)
    own_k = low[:, q:].astype(BF16)
    kk[0, :text] = text_ref[:, q : q + DH]
    kk[0, text:] = own_k
    vv[0, :text, :DH] = text_ref[:, q + DH :]
    vv[0, text:, :DH] = high[:, :DH].astype(BF16)
    for k in range(REACH + 1):
        vv[k, :, DH:] = jnp.ones((rows, DH), BF16)
    tags = seg_ref[...].astype(F32) + 1.0
    tags = jnp.broadcast_to(tags, (8, rows))
    first_tag = tags[0:1, 0:1]
    diag = ones_where(iota((rows, rows), 0) == iota((rows, rows), 1)) * tags[0:1]
    tag_col = dot(diag.astype(BF16), jnp.ones((rows, LANES), BF16))
    pick0 = ones_where(iota((8, DH), 1) == 0).astype(BF16)
    vis_live = ones_where(dot_nt(pick0, own_k)[0:1] < DEAD / 2)
    live_lane = jnp.concatenate([jnp.ones((1, text), F32), vis_live], axis=1)
    a, b = iota((rows, rows), 0), iota((rows, rows), 1)
    tag_wide = jnp.concatenate([tag_col] * (rows // LANES), axis=1)
    seen = (b <= a) & (tag_wide == tags[0:1]) & (live_lane > 0.5)
    own_bias[...] = jnp.where(seen, 0.0, -BIG)
    lane = iota((rows, LANES), 1)
    row_bias = jnp.where(tag_col == first_tag, 0.0, -BIG)
    qx[...] = jnp.where(lane == 0, 1.0, jnp.where(lane == 1, row_bias, 0.0)).astype(BF16)
    live_q = jnp.concatenate(
        [jnp.ones((text, LANES), F32), jnp.broadcast_to(ones_where(low[:, q : q + 1] < DEAD / 2), (vis, LANES))], axis=0
    )
    used = jnp.int32(0)
    place_r = iota((rows, LANES), 0)
    for k in range(1, REACH + 1):
        ref = halos[k - 1]
        got = ref[text : text + 8, :].astype(F32)
        same = ones_where(got == first_tag)
        count = jnp.sum(same[0:1] + same[1:2])
        lo = DH + 2 * DH * (k - 1)
        pk = high[:, lo : lo + DH]
        kk[k, :text] = ref[:text, :DH]
        kk[k, text:] = pk.astype(BF16)
        vv[k, :text, :DH] = ref[:text, DH:]
        vv[k, text:, :DH] = high[:, lo + DH : lo + 2 * DH].astype(BF16)
        live = jnp.concatenate(
            [jnp.ones((text, LANES), F32), jnp.broadcast_to(ones_where(pk[:, 0:1] < DEAD / 2), (vis, LANES))], axis=0
        )
        ok = (place_r >= rows - count.astype(jnp.int32)) & (live > 0.5)
        kx[k] = jnp.where(lane == 0, jnp.where(ok, 0.0, -BIG), ones_where(lane == 1)).astype(BF16)
        used = used + jnp.where(count > 0.5, 1, 0)

    def one_head(h, carry):
        at = pl.multiple_of(h * DH, DH)
        qs = jnp.concatenate([text_ref[:, pl.ds(at, DH)], qv[:, pl.ds(at, DH)]], axis=0)
        s = dot_nt(qs, kk[0]) + own_bias[...]
        ss[0] = s
        top = s[:, :LANES]
        for i in range(1, rows // LANES):
            top = jnp.maximum(top, s[:, i * LANES : (i + 1) * LANES])
        qe = jnp.concatenate([qs, qx[...]], axis=1)

        def score(k, top):
            s = dot_nt(qe, jnp.concatenate([kk[k], kx[k]], axis=1))
            ss[k] = s
            for i in range(rows // LANES):
                top = jnp.maximum(top, s[:, i * LANES : (i + 1) * LANES])
            return top

        top = lax.fori_loop(1, used + 1, score, top)
        top = jnp.max(top, axis=1, keepdims=True)
        top = jnp.broadcast_to(top, (rows, LANES))
        wide = jnp.concatenate([top] * (rows // LANES), axis=1)

        def weigh(k, acc):
            p = jnp.exp2((ss[k] - wide) * SCALE).astype(BF16)
            return acc + dot(p, vv[k])

        acc = weigh(0, jnp.zeros((rows, 2 * DH), F32))
        acc = lax.fori_loop(1, used + 1, weigh, acc)
        out = acc[:, :DH] / acc[:, DH:]
        out_ref[:, pl.ds(at, DH)] = jnp.where(live_q > 0.5, out, 0.0).astype(BF16)
        return carry

    lax.fori_loop(0, GQ, one_head, 0)


def cost(flops, nbytes):
    return pl.CostEstimate(flops=flops, bytes_accessed=nbytes, transcendentals=0)


def shards(text_rows, vis_rows, vis_dest, segments):
    seq_count = lax.axis_size("seq")
    groups = lax.axis_size("group")
    text, _, wide = text_rows.shape
    per_dev, heads, _ = vis_rows.shape
    block = per_dev * heads
    vis = seq_count * CAP
    rows = text + vis
    q = GQ * DH
    total = groups * seq_count

    text2 = text_rows.reshape(text, wide)
    tag = jnp.pad((segments + 1).astype(BF16), (0, 8 * 2 * DH - rows)).reshape(8, 2 * DH)
    mine = jnp.concatenate([text2[:, q:], tag], axis=0)
    pairs = [(o, o + RING) for o in range(total - RING) if o % RING >= RING - REACH]
    ghost = lax.ppermute(mine, ("group", "seq"), pairs)

    listed = pl.pallas_call(
        functools.partial(prep_kernel, per_dev, heads),
        out_shape=jax.ShapeDtypeStruct((block, wide + LANES), BF16),
        name="list_rows",
    )(vis_rows.reshape(block, wide), vis_dest)
    own = lax.all_to_all(listed, "shard", split_axis=0, concat_axis=0, tiled=True)
    tail = pl.pallas_call(
        functools.partial(tail_kernel, (seq_count - REACH) * CAP),
        out_shape=jax.ShapeDtypeStruct((REACH * CAP, 2 * DH), BF16),
        name="pack_tail",
    )(own)
    tail = lax.ppermute(tail, "group", [(i, i + 1) for i in range(groups - 1)])
    packed = pl.pallas_call(
        pack_kernel,
        out_shape=jax.ShapeDtypeStruct((seq_count * 8, DH + 2 * DH * REACH), BF16),
        name="pack_rows",
    )(own, tail)
    came = lax.all_to_all(packed, "seq", split_axis=0, concat_axis=0, tiled=True)

    place_y = lax.axis_index("seq") % RING
    halos = []
    for k in range(1, REACH + 1):
        sent = jnp.where(place_y + k >= RING, ghost, mine)
        ring = [(s, s - s % RING + (s % RING + k) % RING) for s in range(seq_count)]
        halos.append(lax.ppermute(sent, "seq", ring))

    out = pl.pallas_call(
        attend_kernel,
        out_shape=jax.ShapeDtypeStruct((rows, q), BF16),
        scratch_shapes=[
            pltpu.VMEM((vis, q), BF16),
            pltpu.VMEM((REACH + 1, rows, DH), BF16),
            pltpu.VMEM((REACH + 1, rows, LANES), BF16),
            pltpu.VMEM((REACH + 1, rows, 2 * DH), BF16),
            pltpu.VMEM((rows, LANES), BF16),
            pltpu.VMEM((rows, rows), F32),
            pltpu.VMEM((REACH + 1, rows, rows), F32),
        ],
        cost_estimate=cost(6_000_000_000, 4_000_000),
        name="attend",
    )(text2, segments.reshape(1, rows), came, *halos)
    return out.reshape(rows, 1, q)


def solution(mesh):
    placed = (
        P(("group", "seq"), "shard", None),
        P(("group", "seq", "shard"), None, None),
        P(("group", "seq", "shard"), None),
        P(("group", "seq")),
    )
    return jax.shard_map(
        shards,
        mesh=mesh,
        in_specs=placed,
        out_specs=P(("group", "seq"), "shard", None),
        check_vma=False,
    )
```

```python
import functools

import jax
import jax.numpy as jnp
from jax import lax
from jax.experimental import pallas as pl
from jax.experimental.pallas import tpu as pltpu
from jax.sharding import PartitionSpec as P


GQ = 8
DH = 128
CAP = 4
REACH = 4
RING = 8
LANES = 128
DEAD = 64.0
BIG = 1e30
SCALE = DH ** (-0.5) * 1.4426950408889634
F32 = jnp.float32
BF16 = jnp.bfloat16

VARIANTS = (1, 3, 5)


def iota(shape, dim):
    return lax.broadcasted_iota(jnp.int32, shape, dim)


def dot(a, b):
    return jnp.dot(a, b, preferred_element_type=F32)


def dot_nt(a, b):
    return lax.dot_general(a, b, (((1,), (1,)), ((), ())), preferred_element_type=F32)


def ones_where(cond):
    return jnp.where(cond, 1.0, 0.0)


def halo_kernel(text_ref, vis_ref, dest_ref, seg_ref, mine_ref, step_ref):
    text = text_ref.shape[0]
    block = vis_ref.shape[0]
    wide = text_ref.shape[1]
    rows = seg_ref.shape[1]
    per_dev = dest_ref.shape[1]
    mine_ref[:text] = text_ref[...]
    tags = seg_ref[...].astype(F32) + 1.0
    pad = jnp.zeros((1, 2 * wide - rows), F32)
    tags = jnp.concatenate([tags, pad], axis=1)
    tags = jnp.concatenate([tags[:, :wide], tags[:, wide:], jnp.zeros((6, wide), F32)], axis=0)
    mine_ref[text:] = tags.astype(BF16)
    step_ref[:block] = vis_ref[...]
    dest = jnp.concatenate([dest_ref[...].astype(F32), jnp.zeros((1, wide - per_dev), F32)], axis=1)
    step_ref[block:] = jnp.broadcast_to(dest, (8, wide)).astype(BF16)


def list_kernel(per_dev, heads, rows_ref, dest_ref, step_ref, out_ref):
    count = per_dev * heads
    wide = rows_ref.shape[1]
    a, b = iota((count, count), 0), iota((count, count), 1)
    move = ones_where(b == (a % per_dev) * heads + a // per_dev).astype(BF16)
    pick = iota((count, per_dev), 1) == iota((count, per_dev), 0) % per_dev
    dest = jnp.sum(jnp.where(pick, dest_ref[...].astype(F32), 0.0), axis=1, keepdims=True)
    old = jnp.sum(jnp.where(pick, step_ref[count : count + 1, :per_dev].astype(F32), 0.0), axis=1, keepdims=True)
    out_ref[:, :wide] = dot(move, rows_ref[...]).astype(BF16)
    out_ref[:, wide : wide + LANES] = jnp.broadcast_to(dest, (count, LANES)).astype(BF16)
    out_ref[:, wide + LANES : wide + LANES + 2 * DH] = dot(move, step_ref[:count]).astype(BF16)
    out_ref[:, wide + LANES + 2 * DH :] = jnp.broadcast_to(old, (count, LANES)).astype(BF16)


def slot_row(named):
    count = named.shape[0]
    onehot = ones_where(named.astype(F32).astype(jnp.int32) == iota((count, LANES), 1)).astype(BF16)
    same = dot_nt(onehot, onehot)
    a, b = iota((count, count), 0), iota((count, count), 1)
    rank = jnp.sum(jnp.where(a < b, same, 0.0), axis=0, keepdims=True)
    dest = dot_nt(iota((8, LANES), 1).astype(F32).astype(BF16), onehot)[0:1]
    return dest * CAP + rank


def pack_kernel(own_ref, out_ref):
    count = own_ref.shape[0]
    rows = out_ref.shape[0]
    slot_count = rows // 2
    q = GQ * DH
    wide = q + 2 * DH
    slots = slot_row(own_ref[:, wide : wide + LANES])
    before = slot_row(own_ref[:, wide + LANES + 2 * DH :]) - slot_count
    both = jnp.concatenate([slots, before], axis=1)
    kv = jnp.concatenate([own_ref[:, q:wide], own_ref[:, wide + LANES : wide + LANES + 2 * DH]], axis=0)
    r = iota((rows, count), 0)
    sid = ((r // 8) * CAP + r % CAP).astype(F32)
    low = (r % 8) < CAP
    put0 = ones_where(low & (sid == slots))
    put1 = ones_where((~low) & (sid == slots))
    base = dot(put0.astype(BF16), own_ref[:, : q + DH])
    fill0 = jnp.sum(put0, axis=1, keepdims=True)
    first = base[:, :DH] + dot(put1.astype(BF16), own_ref[:, q + DH : wide])
    fill = fill0 + jnp.sum(put1, axis=1, keepdims=True)
    out_ref[:, :DH] = jnp.where(fill > 0, first, DEAD).astype(BF16)
    r = iota((rows, 2 * count), 0)
    sid = ((r // 8) * CAP + r % CAP).astype(F32)
    low = (r % 8) < CAP
    for k in range(1, REACH + 1):
        put = ones_where((~low) & (sid - CAP * k == both))
        lo = DH + 2 * DH * (k - 1)
        val = base[:, lo : lo + 2 * DH] + dot(put.astype(BF16), kv)
        fill = fill0 + jnp.sum(put, axis=1, keepdims=True)
        out_ref[:, lo : lo + 2 * DH] = jnp.where(fill > 0, val, DEAD).astype(BF16)


def attend_kernel(text_ref, seg_ref, came_ref, b1, b2, b3, far, c1, c2, c3, out_ref, qv, kk, vv, qx, own_bias, sa, sb):
    text = text_ref.shape[0]
    vis = came_ref.shape[0] // 2
    rows = text + vis
    q = GQ * DH
    a, b = iota((vis, 2 * vis), 0), iota((vis, 2 * vis), 1)
    src = (a // CAP) * 8 + a % CAP
    low = dot(ones_where(b == src).astype(BF16), came_ref[...])
    high = dot(ones_where(b == src + CAP).astype(BF16), came_ref[...])
    qv[...] = low[:, :q].astype(BF16)
    own_k = low[:, q:].astype(BF16)
    kk[:text, :DH] = text_ref[:, q : q + DH]
    kk[text:rows, :DH] = own_k
    kk[:rows, DH:] = jnp.zeros((rows, LANES), BF16)
    vv[:text, :DH] = text_ref[:, q + DH :]
    vv[text:rows, :DH] = high[:, :DH].astype(BF16)
    vv[:, DH:] = jnp.ones((vv.shape[0], DH), BF16)
    tags = jnp.broadcast_to(seg_ref[0:1].astype(F32) + 1.0, (8, rows))
    first_tag = tags[0:1, 0:1]
    diag = ones_where(iota((rows, rows), 0) == iota((rows, rows), 1)) * tags[0:1]
    tag_col = dot(diag.astype(BF16), jnp.ones((rows, LANES), BF16))
    pick0 = ones_where(iota((8, DH), 1) == 0).astype(BF16)
    vis_live = ones_where(dot_nt(pick0, own_k)[0:1] < DEAD / 2)
    live_lane = jnp.concatenate([jnp.ones((1, text), F32), vis_live], axis=1)
    a, b = iota((rows, rows), 0), iota((rows, rows), 1)
    tag_wide = jnp.concatenate([tag_col] * (rows // LANES), axis=1)
    seen = (b <= a) & (tag_wide == tags[0:1]) & (live_lane > 0.5)
    own_bias[...] = jnp.where(seen, 0.0, -BIG)
    lane = iota((rows, LANES), 1)
    row_bias = jnp.where(tag_col == first_tag, 0.0, -BIG)
    qx[...] = jnp.where(lane == 0, 1.0, jnp.where(lane == 1, row_bias, 0.0)).astype(BF16)
    live_q = jnp.concatenate(
        [jnp.ones((text, LANES), F32), jnp.broadcast_to(ones_where(low[:, q : q + 1] < DEAD / 2), (vis, LANES))], axis=0
    )
    used = jnp.int32(0)
    place_r = iota((rows, LANES), 0)
    for k in range(1, REACH + 1):
        ref = far[...] if k == REACH else (b1, b2, b3)[k - 1][...] + (c1, c2, c3)[k - 1][...]
        got = ref[text : text + 8, :].astype(F32)
        same = ones_where(got == first_tag)
        count = jnp.sum(same[0:1] + same[1:2])
        at = k * rows
        lo = DH + 2 * DH * (k - 1)
        pk = high[:, lo : lo + DH]
        kk[at : at + text, :DH] = ref[:text, :DH]
        kk[at + text : at + rows, :DH] = pk.astype(BF16)
        vv[at : at + text, :DH] = ref[:text, DH:]
        vv[at + text : at + rows, :DH] = high[:, lo + DH : lo + 2 * DH].astype(BF16)
        live = jnp.concatenate(
            [jnp.ones((text, LANES), F32), jnp.broadcast_to(ones_where(pk[:, 0:1] < DEAD / 2), (vis, LANES))], axis=0
        )
        ok = (place_r >= rows - count.astype(jnp.int32)) & (live > 0.5)
        kk[at : at + rows, DH:] = jnp.where(lane == 0, jnp.where(ok, 0.0, -BIG), ones_where(lane == 1)).astype(BF16)
        used = used + jnp.where(count > 0.5, 1, 0)

    def score(h, blocks, ss):
        at = pl.multiple_of(h * DH, DH)
        qs = jnp.concatenate([text_ref[:, pl.ds(at, DH)], qv[:, pl.ds(at, DH)]], axis=0)
        qe = jnp.concatenate([qs, qx[...]], axis=1)
        top = None
        for k in range(blocks):
            s = dot_nt(qe, kk[k * rows : (k + 1) * rows])
            if k == 0:
                s = s + own_bias[...]
            ss[:, k * rows : (k + 1) * rows] = s
            for i in range(rows // LANES):
                part = s[:, i * LANES : (i + 1) * LANES]
                top = part if top is None else jnp.maximum(top, part)
        return jnp.max(top, axis=1, keepdims=True)

    def weigh(h, blocks, ss, top):
        at = pl.multiple_of(h * DH, DH)
        p = jnp.exp2((ss[:, : blocks * rows] - top) * SCALE).astype(BF16)
        acc = dot(p, vv[: blocks * rows])
        out = acc[:, :DH] / acc[:, DH:]
        out_ref[:, pl.ds(at, DH)] = jnp.where(live_q > 0.5, out, 0.0).astype(BF16)

    def run(blocks):
        def two(i, top):
            h = 2 * i
            after = score(h + 1, blocks, sb)
            weigh(h, blocks, sa, top)
            top = score(jnp.minimum(h + 2, GQ - 1), blocks, sa)
            weigh(h + 1, blocks, sb, after)
            return top

        lax.fori_loop(0, GQ // 2, two, score(0, blocks, sa))

    for blocks in VARIANTS:
        lower = max([b for b in VARIANTS if b < blocks], default=0)

        @pl.when((used + 1 > lower) & (used + 1 <= blocks))
        def _(blocks=blocks):
            run(blocks)


def cost(flops, nbytes):
    return pl.CostEstimate(flops=flops, bytes_accessed=nbytes, transcendentals=0)


def vmem(mib):
    return pltpu.CompilerParams(vmem_limit_bytes=mib << 20)


def layer(text_rows, vis_rows, vis_dest, segments):
    seq_count = lax.axis_size("seq")
    groups = lax.axis_size("group")
    text, _, wide = text_rows.shape
    per_dev, heads, _ = vis_rows.shape
    block = per_dev * heads
    vis = seq_count * CAP
    rows = text + vis
    q = GQ * DH
    total = groups * seq_count

    text2 = text_rows.reshape(text, wide)
    vis2 = vis_rows.reshape(block, wide)
    dest = vis_dest.reshape(1, per_dev)
    tail_block = q // (2 * DH)
    mine, step = pl.pallas_call(
        halo_kernel,
        grid=(1,),
        in_specs=[
            pl.BlockSpec((text, 2 * DH), lambda i: (0, tail_block)),
            pl.BlockSpec((block, 2 * DH), lambda i: (0, tail_block)),
            pl.BlockSpec((1, per_dev), lambda i: (0, 0)),
            pl.BlockSpec((1, rows), lambda i: (0, 0)),
        ],
        out_specs=[
            pl.BlockSpec((text + 8, 2 * DH), lambda i: (0, 0)),
            pl.BlockSpec((block + 8, 2 * DH), lambda i: (0, 0)),
        ],
        out_shape=[
            jax.ShapeDtypeStruct((text + 8, 2 * DH), BF16),
            jax.ShapeDtypeStruct((block + 8, 2 * DH), BF16),
        ],
        cost_estimate=cost(1000, 300_000),
        compiler_params=vmem(8),
        name="halo_rows",
    )(text2, vis2, dest, segments.reshape(1, rows))
    step = lax.ppermute(step, "group", [(i, i + 1) for i in range(groups - 1)])

    far = lax.ppermute(mine, ("group", "seq"), [(o, o + REACH) for o in range(total - REACH)])
    near, seam = [], []
    for k in range(1, REACH):
        pairs = [(s, s + k) for s in range(seq_count) if s % RING + k < RING]
        near.append(lax.ppermute(mine, "seq", pairs))
    for k in range(1, REACH):
        pairs = [(s + REACH - k, s) for s in range(seq_count) if s % RING < k]
        seam.append(lax.ppermute(far, "seq", pairs))

    listed = pl.pallas_call(
        functools.partial(list_kernel, per_dev, heads),
        out_shape=jax.ShapeDtypeStruct((block, wide + 2 * DH + 2 * LANES), BF16),
        cost_estimate=cost(15_000_000, 400_000),
        compiler_params=vmem(8),
        name="list_rows",
    )(vis2, dest, step)
    own = lax.all_to_all(listed, "shard", split_axis=0, concat_axis=0, tiled=True)

    packed = pl.pallas_call(
        pack_kernel,
        out_shape=jax.ShapeDtypeStruct((seq_count * 8, DH + 2 * DH * REACH), BF16),
        cost_estimate=cost(200_000_000, 800_000),
        compiler_params=vmem(12),
        name="pack_rows",
    )(own)
    came = lax.all_to_all(packed, "seq", split_axis=0, concat_axis=0, tiled=True)

    out = pl.pallas_call(
        attend_kernel,
        out_shape=jax.ShapeDtypeStruct((rows, q), BF16),
        scratch_shapes=[
            pltpu.VMEM((vis, q), BF16),
            pltpu.VMEM(((REACH + 1) * rows, DH + LANES), BF16),
            pltpu.VMEM(((REACH + 1) * rows, 2 * DH), BF16),
            pltpu.VMEM((rows, LANES), BF16),
            pltpu.VMEM((rows, rows), F32),
            pltpu.VMEM((rows, (REACH + 1) * rows), F32),
            pltpu.VMEM((rows, (REACH + 1) * rows), F32),
        ],
        cost_estimate=cost(6_000_000_000, 4_000_000),
        compiler_params=vmem(32),
        name="attend",
    )(text2, segments.reshape(1, rows), came, *near, far, *seam)
    return out.reshape(rows, 1, q)


def solution(mesh):
    placed = (
        P(("group", "seq"), "shard", None),
        P(("group", "seq", "shard"), None, None),
        P(("group", "seq", "shard"), None),
        P(("group", "seq")),
    )
    return jax.shard_map(
        layer,
        mesh=mesh,
        in_specs=placed,
        out_specs=P(("group", "seq"), "shard", None),
        check_vma=False,
    )
```

```python
import functools

import jax
import jax.numpy as jnp
from jax import lax
from jax.experimental import pallas as pl
from jax.experimental.pallas import tpu as pltpu
from jax.sharding import PartitionSpec as P


GQ = 8
DH = 128
CAP = 4
REACH = 4
RING = 8
LANES = 128
DEAD = 64.0
BIG = 1e30
SCALE = DH ** (-0.5) * 1.4426950408889634
F32 = jnp.float32
BF16 = jnp.bfloat16

VARIANTS = (1, 2, 3, 4, 5)


def iota(shape, dim):
    return lax.broadcasted_iota(jnp.int32, shape, dim)


def dot(a, b):
    return jnp.dot(a, b, preferred_element_type=F32)


def dot_nt(a, b):
    return lax.dot_general(a, b, (((1,), (1,)), ((), ())), preferred_element_type=F32)


def ones_where(cond):
    return jnp.where(cond, 1.0, 0.0)


def seg_lanes(seg_ref):
    return jnp.concatenate([seg_ref[i : i + 1] for i in range(seg_ref.shape[0])], axis=1).astype(F32)


def halo_kernel(text_ref, seg_ref, mine_ref):
    text, wide = text_ref.shape
    mine_ref[:text] = text_ref[...]
    tags = seg_lanes(seg_ref) + 1.0
    pad = jnp.zeros((1, 2 * wide - tags.shape[1]), F32)
    tags = jnp.concatenate([tags, pad], axis=1)
    tags = jnp.concatenate([tags[:, :wide], tags[:, wide:], jnp.zeros((6, wide), F32)], axis=0)
    mine_ref[text:] = tags.astype(BF16)


def step_kernel(vis_ref, dest_ref, step_ref):
    block, wide = vis_ref.shape
    per_dev = dest_ref.shape[1]
    step_ref[:block] = vis_ref[...]
    dest = jnp.concatenate([dest_ref[...].astype(F32), jnp.zeros((1, wide - per_dev), F32)], axis=1)
    step_ref[block:] = jnp.broadcast_to(dest, (8, wide)).astype(BF16)


def list_kernel(per_dev, heads, rows_ref, dest_ref, step_ref, out_ref):
    count = per_dev * heads
    wide = rows_ref.shape[1]
    a, b = iota((count, count), 0), iota((count, count), 1)
    move = ones_where(b == (a % per_dev) * heads + a // per_dev).astype(BF16)
    pick = iota((count, per_dev), 1) == iota((count, per_dev), 0) % per_dev
    dest = jnp.sum(jnp.where(pick, dest_ref[...].astype(F32), 0.0), axis=1, keepdims=True)
    old = jnp.sum(jnp.where(pick, step_ref[count : count + 1, :per_dev].astype(F32), 0.0), axis=1, keepdims=True)
    out_ref[:, :wide] = dot(move, rows_ref[...]).astype(BF16)
    out_ref[:, wide : wide + LANES] = jnp.broadcast_to(dest, (count, LANES)).astype(BF16)
    out_ref[:, wide + LANES : wide + LANES + 2 * DH] = dot(move, step_ref[:count]).astype(BF16)
    out_ref[:, wide + LANES + 2 * DH :] = jnp.broadcast_to(old, (count, LANES)).astype(BF16)


def slot_row(named):
    count = named.shape[0]
    onehot = ones_where(named.astype(F32).astype(jnp.int32) == iota((count, LANES), 1)).astype(BF16)
    same = dot_nt(onehot, onehot)
    a, b = iota((count, count), 0), iota((count, count), 1)
    rank = jnp.sum(jnp.where(a < b, same, 0.0), axis=0, keepdims=True)
    dest = dot_nt(iota((8, LANES), 1).astype(F32).astype(BF16), onehot)[0:1]
    return dest * CAP + rank


def pack_kernel(own_ref, out_ref):
    count = own_ref.shape[0]
    rows = out_ref.shape[0]
    slot_count = rows // 2
    q = GQ * DH
    wide = q + 2 * DH
    slots = slot_row(own_ref[:, wide : wide + LANES])
    before = slot_row(own_ref[:, wide + LANES + 2 * DH :]) - slot_count
    both = jnp.concatenate([slots, before], axis=1)
    kv = jnp.concatenate([own_ref[:, q:wide], own_ref[:, wide + LANES : wide + LANES + 2 * DH]], axis=0)
    r = iota((rows, count), 0)
    sid = ((r // 8) * CAP + r % CAP).astype(F32)
    low = (r % 8) < CAP
    put0 = ones_where(low & (sid == slots))
    put1 = ones_where((~low) & (sid == slots))
    base = dot(put0.astype(BF16), own_ref[:, : q + DH])
    fill0 = jnp.sum(put0, axis=1, keepdims=True)
    first = base[:, :DH] + dot(put1.astype(BF16), own_ref[:, q + DH : wide])
    fill = fill0 + jnp.sum(put1, axis=1, keepdims=True)
    out_ref[:, :DH] = jnp.where(fill > 0, first, DEAD).astype(BF16)
    r = iota((rows, 2 * count), 0)
    sid = ((r // 8) * CAP + r % CAP).astype(F32)
    low = (r % 8) < CAP
    for k in range(1, REACH + 1):
        put = ones_where((~low) & (sid - CAP * k == both))
        lo = DH + 2 * DH * (k - 1)
        val = base[:, lo : lo + 2 * DH] + dot(put.astype(BF16), kv)
        fill = fill0 + jnp.sum(put, axis=1, keepdims=True)
        out_ref[:, lo : lo + 2 * DH] = jnp.where(fill > 0, val, DEAD).astype(BF16)


def attend_kernel(text_ref, seg_ref, came_ref, b1, b2, b3, far, c1, c2, c3, out_ref, qv, kk, vv, qx, own_bias, sa, sb):
    text = text_ref.shape[0]
    vis = came_ref.shape[0] // 2
    rows = text + vis
    q = GQ * DH
    a, b = iota((vis, 2 * vis), 0), iota((vis, 2 * vis), 1)
    src = (a // CAP) * 8 + a % CAP
    low = dot(ones_where(b == src).astype(BF16), came_ref[...])
    high = dot(ones_where(b == src + CAP).astype(BF16), came_ref[...])
    qv[...] = low[:, :q].astype(BF16)
    own_k = low[:, q:].astype(BF16)
    kk[:text, :DH] = text_ref[:, q : q + DH]
    kk[text:rows, :DH] = own_k
    kk[:rows, DH:] = jnp.zeros((rows, LANES), BF16)
    vv[:text, :DH] = text_ref[:, q + DH :]
    vv[text:rows, :DH] = high[:, :DH].astype(BF16)
    vv[:, DH:] = jnp.ones((vv.shape[0], DH), BF16)
    tags = jnp.broadcast_to(seg_lanes(seg_ref) + 1.0, (8, rows))
    first_tag = tags[0:1, 0:1]
    diag = ones_where(iota((rows, rows), 0) == iota((rows, rows), 1)) * tags[0:1]
    tag_col = dot(diag.astype(BF16), jnp.ones((rows, LANES), BF16))
    pick0 = ones_where(iota((8, DH), 1) == 0).astype(BF16)
    vis_live = ones_where(dot_nt(pick0, own_k)[0:1] < DEAD / 2)
    live_lane = jnp.concatenate([jnp.ones((1, text), F32), vis_live], axis=1)
    a, b = iota((rows, rows), 0), iota((rows, rows), 1)
    tag_wide = jnp.concatenate([tag_col] * (rows // LANES), axis=1)
    seen = (b <= a) & (tag_wide == tags[0:1]) & (live_lane > 0.5)
    own_bias[...] = jnp.where(seen, 0.0, -BIG)
    lane = iota((rows, LANES), 1)
    row_bias = jnp.where(tag_col == first_tag, 0.0, -BIG)
    qx[...] = jnp.where(lane == 0, 1.0, jnp.where(lane == 1, row_bias, 0.0)).astype(BF16)
    live_q = jnp.concatenate(
        [jnp.ones((text, LANES), F32), jnp.broadcast_to(ones_where(low[:, q : q + 1] < DEAD / 2), (vis, LANES))], axis=0
    )
    used = jnp.int32(0)
    place_r = iota((rows, LANES), 0)
    for k in range(1, REACH + 1):
        ref = far[...] if k == REACH else (b1, b2, b3)[k - 1][...] + (c1, c2, c3)[k - 1][...]
        got = ref[text : text + 8, :].astype(F32)
        same = ones_where(got == first_tag)
        count = jnp.sum(same[0:1] + same[1:2])
        at = k * rows
        lo = DH + 2 * DH * (k - 1)
        pk = high[:, lo : lo + DH]
        kk[at : at + text, :DH] = ref[:text, :DH]
        kk[at + text : at + rows, :DH] = pk.astype(BF16)
        vv[at : at + text, :DH] = ref[:text, DH:]
        vv[at + text : at + rows, :DH] = high[:, lo + DH : lo + 2 * DH].astype(BF16)
        live = jnp.concatenate(
            [jnp.ones((text, LANES), F32), jnp.broadcast_to(ones_where(pk[:, 0:1] < DEAD / 2), (vis, LANES))], axis=0
        )
        ok = (place_r >= rows - count.astype(jnp.int32)) & (live > 0.5)
        kk[at : at + rows, DH:] = jnp.where(lane == 0, jnp.where(ok, 0.0, -BIG), ones_where(lane == 1)).astype(BF16)
        used = used + jnp.where(count > 0.5, 1, 0)

    def score(h, blocks, ss):
        at = pl.multiple_of(h * DH, DH)
        qs = jnp.concatenate([text_ref[:, pl.ds(at, DH)], qv[:, pl.ds(at, DH)]], axis=0)
        qe = jnp.concatenate([qs, qx[...]], axis=1)
        top = None
        for k in range(blocks):
            s = dot_nt(qe, kk[k * rows : (k + 1) * rows])
            if k == 0:
                s = s + own_bias[...]
            ss[:, k * rows : (k + 1) * rows] = s
            for i in range(rows // LANES):
                part = s[:, i * LANES : (i + 1) * LANES]
                top = part if top is None else jnp.maximum(top, part)
        return jnp.max(top, axis=1, keepdims=True)

    def weigh(h, blocks, ss, top):
        at = pl.multiple_of(h * DH, DH)
        p = jnp.exp2((ss[:, : blocks * rows] - top) * SCALE).astype(BF16)
        acc = dot(p, vv[: blocks * rows])
        out = acc[:, :DH] / acc[:, DH:]
        out_ref[:, pl.ds(at, DH)] = jnp.where(live_q > 0.5, out, 0.0).astype(BF16)

    def run(blocks):
        def two(i, top):
            h = 2 * i
            after = score(h + 1, blocks, sb)
            weigh(h, blocks, sa, top)
            top = score(jnp.minimum(h + 2, GQ - 1), blocks, sa)
            weigh(h + 1, blocks, sb, after)
            return top

        lax.fori_loop(0, GQ // 2, two, score(0, blocks, sa))

    for blocks in VARIANTS:
        lower = max([b for b in VARIANTS if b < blocks], default=0)

        @pl.when((used + 1 > lower) & (used + 1 <= blocks))
        def _(blocks=blocks):
            run(blocks)


def cost(flops, nbytes):
    return pl.CostEstimate(flops=flops, bytes_accessed=nbytes, transcendentals=0)


def vmem(mib):
    return pltpu.CompilerParams(vmem_limit_bytes=mib << 20)


def layer(text_rows, vis_rows, vis_dest, segments):
    seq_count = lax.axis_size("seq")
    groups = lax.axis_size("group")
    text, _, wide = text_rows.shape
    per_dev, heads, _ = vis_rows.shape
    block = per_dev * heads
    vis = seq_count * CAP
    rows = text + vis
    q = GQ * DH
    total = groups * seq_count

    text2 = text_rows.reshape(text, wide)
    vis2 = vis_rows.reshape(block, wide)
    dest = vis_dest.reshape(1, per_dev)
    segs = segments.reshape(rows // LANES, LANES)
    tail_block = q // (2 * DH)
    step = pl.pallas_call(
        step_kernel,
        grid=(1,),
        in_specs=[
            pl.BlockSpec((block, 2 * DH), lambda i: (0, tail_block)),
            pl.BlockSpec((1, per_dev), lambda i: (0, 0)),
        ],
        out_specs=pl.BlockSpec((block + 8, 2 * DH), lambda i: (0, 0)),
        out_shape=jax.ShapeDtypeStruct((block + 8, 2 * DH), BF16),
        cost_estimate=cost(1000, 70_000),
        name="step_rows",
    )(vis2, dest)
    mine = pl.pallas_call(
        halo_kernel,
        grid=(1,),
        in_specs=[
            pl.BlockSpec((text, 2 * DH), lambda i: (0, tail_block)),
            pl.BlockSpec((rows // LANES, LANES), lambda i: (0, 0)),
        ],
        out_specs=pl.BlockSpec((text + 8, 2 * DH), lambda i: (0, 0)),
        out_shape=jax.ShapeDtypeStruct((text + 8, 2 * DH), BF16),
        cost_estimate=cost(1000, 300_000),
        name="halo_rows",
    )(text2, segs)
    step = lax.ppermute(step, "group", [(i, i + 1) for i in range(groups - 1)])

    far = lax.ppermute(mine, ("group", "seq"), [(o, o + REACH) for o in range(total - REACH)])
    near, seam = [], []
    for k in range(1, REACH):
        by = 1 if k == REACH - 1 else k
        pairs = [(s, s + by) for s in range(seq_count) if s % RING + by < RING]
        near.append(lax.ppermute(near[-1] if by < k else mine, "seq", pairs))
    for k in range(1, REACH):
        pairs = [(s + REACH - k, s) for s in range(seq_count) if s % RING < k]
        seam.append(lax.ppermute(far, "seq", pairs))

    listed = pl.pallas_call(
        functools.partial(list_kernel, per_dev, heads),
        out_shape=jax.ShapeDtypeStruct((block, wide + 2 * DH + 2 * LANES), BF16),
        cost_estimate=cost(15_000_000, 400_000),
        compiler_params=vmem(8),
        name="list_rows",
    )(vis2, dest, step)
    own = lax.all_to_all(listed, "shard", split_axis=0, concat_axis=0, tiled=True)

    packed = pl.pallas_call(
        pack_kernel,
        out_shape=jax.ShapeDtypeStruct((seq_count * 8, DH + 2 * DH * REACH), BF16),
        cost_estimate=cost(200_000_000, 800_000),
        compiler_params=vmem(12),
        name="pack_rows",
    )(own)
    came = lax.all_to_all(packed, "seq", split_axis=0, concat_axis=0, tiled=True)

    out = pl.pallas_call(
        attend_kernel,
        out_shape=jax.ShapeDtypeStruct((rows, q), BF16),
        scratch_shapes=[
            pltpu.VMEM((vis, q), BF16),
            pltpu.VMEM(((REACH + 1) * rows, DH + LANES), BF16),
            pltpu.VMEM(((REACH + 1) * rows, 2 * DH), BF16),
            pltpu.VMEM((rows, LANES), BF16),
            pltpu.VMEM((rows, rows), F32),
            pltpu.VMEM((rows, (REACH + 1) * rows), F32),
            pltpu.VMEM((rows, (REACH + 1) * rows), F32),
        ],
        cost_estimate=cost(6_000_000_000, 4_000_000),
        compiler_params=vmem(32),
        name="attend",
    )(text2, segs, came, *near, far, *seam)
    return out.reshape(rows, 1, q)


def solution(mesh):
    placed = (
        P(("group", "seq"), "shard", None),
        P(("group", "seq", "shard"), None, None),
        P(("group", "seq", "shard"), None),
        P(("group", "seq")),
    )
    return jax.shard_map(
        layer,
        mesh=mesh,
        in_specs=placed,
        out_specs=P(("group", "seq"), "shard", None),
        check_vma=False,
    )
```

```python
import functools

import jax
import jax.numpy as jnp
from jax import lax
from jax.experimental import pallas as pl
from jax.experimental.pallas import tpu as pltpu
from jax.sharding import PartitionSpec as P


GQ = 8
DH = 128
CAP = 4
REACH = 4
RING = 8
LANES = 128
DEAD = 64.0
BIG = 1e30
SCALE = DH ** (-0.5) * 1.4426950408889634
F32 = jnp.float32
BF16 = jnp.bfloat16


def iota(shape, dim):
    return lax.broadcasted_iota(jnp.int32, shape, dim)


def dot(a, b):
    return jnp.dot(a, b, preferred_element_type=F32)


def dot_nt(a, b):
    return lax.dot_general(a, b, (((1,), (1,)), ((), ())), preferred_element_type=F32)


def ones_where(cond):
    return jnp.where(cond, 1.0, 0.0)


def seg_lanes(seg_ref):
    return jnp.concatenate([seg_ref[i : i + 1] for i in range(seg_ref.shape[0])], axis=1).astype(F32)


def halo_kernel(text_ref, seg_ref, mine_ref):
    text, wide = text_ref.shape
    mine_ref[:text] = text_ref[...]
    tags = seg_lanes(seg_ref) + 1.0
    pad = jnp.zeros((1, 2 * wide - tags.shape[1]), F32)
    tags = jnp.concatenate([tags, pad], axis=1)
    tags = jnp.concatenate([tags[:, :wide], tags[:, wide:], jnp.zeros((6, wide), F32)], axis=0)
    mine_ref[text:] = tags.astype(BF16)


def step_kernel(vis_ref, dest_ref, step_ref):
    block, wide = vis_ref.shape
    per_dev = dest_ref.shape[1]
    step_ref[:block] = vis_ref[...]
    dest = jnp.concatenate([dest_ref[...].astype(F32), jnp.zeros((1, wide - per_dev), F32)], axis=1)
    step_ref[block:] = jnp.broadcast_to(dest, (8, wide)).astype(BF16)


def row_move(per_dev, heads):
    count = per_dev * heads
    a, b = iota((count, count), 0), iota((count, count), 1)
    move = ones_where(b == (a % per_dev) * heads + a // per_dev).astype(BF16)
    return move, iota((count, per_dev), 1) == iota((count, per_dev), 0) % per_dev


def spread(pick, dest):
    dest = jnp.sum(jnp.where(pick, dest, 0.0), axis=1, keepdims=True)
    return jnp.broadcast_to(dest, (pick.shape[0], LANES)).astype(BF16)


def list_kernel(per_dev, heads, rows_ref, dest_ref, out_ref):
    wide = rows_ref.shape[1]
    move, pick = row_move(per_dev, heads)
    out_ref[:, :wide] = dot(move, rows_ref[...]).astype(BF16)
    out_ref[:, wide : wide + LANES] = spread(pick, dest_ref[...].astype(F32))


def add_kernel(per_dev, heads, step_ref, listed_ref, out_ref):
    count = per_dev * heads
    wide = listed_ref.shape[1]
    move, pick = row_move(per_dev, heads)
    out_ref[:, :wide] = listed_ref[...]
    out_ref[:, wide : wide + 2 * DH] = dot(move, step_ref[:count]).astype(BF16)
    out_ref[:, wide + 2 * DH :] = spread(pick, step_ref[count : count + 1, :per_dev].astype(F32))


def slot_row(named):
    count = named.shape[0]
    onehot = ones_where(named.astype(F32).astype(jnp.int32) == iota((count, LANES), 1)).astype(BF16)
    same = dot_nt(onehot, onehot)
    a, b = iota((count, count), 0), iota((count, count), 1)
    rank = jnp.sum(jnp.where(a < b, same, 0.0), axis=0, keepdims=True)
    dest = dot_nt(iota((8, LANES), 1).astype(F32).astype(BF16), onehot)[0:1]
    return dest * CAP + rank


def pack_kernel(own_ref, out_ref):
    count = own_ref.shape[0]
    rows = out_ref.shape[0]
    slot_count = rows // 2
    q = GQ * DH
    wide = q + 2 * DH
    slots = slot_row(own_ref[:, wide : wide + LANES])
    before = slot_row(own_ref[:, wide + LANES + 2 * DH :]) - slot_count
    both = jnp.concatenate([slots, before], axis=1)
    kv = jnp.concatenate([own_ref[:, q:wide], own_ref[:, wide + LANES : wide + LANES + 2 * DH]], axis=0)
    r = iota((rows, count), 0)
    sid = ((r // 8) * CAP + r % CAP).astype(F32)
    low = (r % 8) < CAP
    put0 = ones_where(low & (sid == slots))
    put1 = ones_where((~low) & (sid == slots))
    base = dot(put0.astype(BF16), own_ref[:, : q + DH])
    fill0 = jnp.sum(put0, axis=1, keepdims=True)
    first = base[:, :DH] + dot(put1.astype(BF16), own_ref[:, q + DH : wide])
    fill = fill0 + jnp.sum(put1, axis=1, keepdims=True)
    out_ref[:, :DH] = jnp.where(fill > 0, first, DEAD).astype(BF16)
    r = iota((rows, 2 * count), 0)
    sid = ((r // 8) * CAP + r % CAP).astype(F32)
    low = (r % 8) < CAP
    for k in range(1, REACH + 1):
        put = ones_where((~low) & (sid - CAP * k == both))
        lo = DH + 2 * DH * (k - 1)
        val = base[:, lo : lo + 2 * DH] + dot(put.astype(BF16), kv)
        fill = fill0 + jnp.sum(put, axis=1, keepdims=True)
        out_ref[:, lo : lo + 2 * DH] = jnp.where(fill > 0, val, DEAD).astype(BF16)


def by_blocks(used, run):
    for blocks in range(1, REACH + 2):

        @pl.when(used + 1 == blocks)
        def _(blocks=blocks):
            run(blocks)


PAIR = 2


def over_pairs(score, weigh, bufs):
    count = GQ // PAIR

    def two(i, top):
        u = 2 * i
        after = score(u + 1, bufs[1])
        weigh(u, bufs[0], top)
        top = score(jnp.minimum(u + 2, count - 1), bufs[0])
        weigh(u + 1, bufs[1], after)
        return top

    lax.fori_loop(0, count // 2, two, score(0, bufs[0]))


def pair_rows(ref, u, extra):
    got = ref[:, pl.ds(pl.multiple_of(u * PAIR * DH, PAIR * DH), PAIR * DH)]
    both = jnp.concatenate([got[:, :DH], got[:, DH:]], axis=0)
    return jnp.concatenate([both, jnp.concatenate([extra, extra], axis=0)], axis=1)


def twice(x):
    return jnp.concatenate([x, x], axis=0)


def row_max(parts):
    top = None
    for s in parts:
        for i in range(s.shape[1] // LANES):
            part = s[:, i * LANES : (i + 1) * LANES]
            top = part if top is None else jnp.maximum(top, part)
    return jnp.max(top, axis=1, keepdims=True)


def text_kernel(
    text_ref, seg_ref, b1, b2, b3, far, c1, c2, c3, part_ref, ml_ref, kvt, qx, bias_ref, counts_ref, kt, vt, bias_t, sa, sb
):
    text = text_ref.shape[0]
    rows = qx.shape[0]
    vis = rows - text
    q = GQ * DH
    kt[:text, :DH] = text_ref[:, q : q + DH]
    kt[:text, DH:] = jnp.zeros((text, LANES), BF16)
    vt[:text, :DH] = text_ref[:, q + DH :]
    vt[:, DH:] = jnp.ones((vt.shape[0], DH), BF16)
    kvt[:text] = text_ref[:, q:]
    tags = jnp.broadcast_to(seg_lanes(seg_ref) + 1.0, (8, rows))
    first_tag = tags[0:1, 0:1]
    diag = ones_where(iota((rows, rows), 0) == iota((rows, rows), 1)) * tags[0:1]
    tag_col = dot(diag.astype(BF16), jnp.ones((rows, LANES), BF16))
    a, b = iota((text, text), 0), iota((text, text), 1)
    wide = jnp.concatenate([tag_col[:text]] * (text // LANES), axis=1)
    bias_t[...] = jnp.where((b <= a) & (wide == tags[0:1, :text]), 0.0, -BIG)
    a, b = iota((vis, rows), 0) + text, iota((vis, rows), 1)
    wide = jnp.concatenate([tag_col[text:]] * (rows // LANES), axis=1)
    bias_ref[...] = jnp.where((b <= a) & (wide == tags[0:1]), 0.0, -BIG)
    lane = iota((rows, LANES), 1)
    row_bias = jnp.where(tag_col == first_tag, 0.0, -BIG)
    qx[...] = jnp.where(lane == 0, 1.0, jnp.where(lane == 1, row_bias, 0.0)).astype(BF16)
    place_r = iota((text, LANES), 0).astype(F32)
    counts = []
    for k in range(1, REACH + 1):
        ref = far[...] if k == REACH else (b1, b2, b3)[k - 1][...] + (c1, c2, c3)[k - 1][...]
        same = ones_where(ref[text : text + 8, :].astype(F32) == first_tag)
        count = jnp.sum(same[0:1] + same[1:2], axis=1, keepdims=True)
        at = k * text
        kt[at : at + text, :DH] = ref[:text, :DH]
        vt[at : at + text, :DH] = ref[:text, DH:]
        kvt[at : at + text] = ref[:text]
        ok = jnp.where(place_r >= rows - count, 0.0, -BIG)
        kt[at : at + text, DH:] = jnp.where(lane[:text] == 0, ok, ones_where(lane[:text] == 1)).astype(BF16)
        counts.append(jnp.broadcast_to(count, (1, LANES)))
    counts = jnp.concatenate(counts + [jnp.zeros((8 - REACH, LANES), F32)], axis=0)
    counts_ref[...] = counts
    used = jnp.sum(ones_where(counts[:, :1] > 0.5)).astype(jnp.int32)

    def run(blocks):
        def score(u, ss):
            qe = pair_rows(text_ref, u, qx[:text])
            parts = []
            for k in range(blocks):
                s = dot_nt(qe, kt[k * text : (k + 1) * text])
                if k == 0:
                    s = s + twice(bias_t[...])
                ss[:, k * text : (k + 1) * text] = s
                parts.append(s)
            return row_max(parts)

        def weigh(u, ss, top):
            p = jnp.exp2((ss[:, : blocks * text] - top) * SCALE).astype(BF16)
            acc = dot(p, vt[: blocks * text])
            at = pl.multiple_of(u * PAIR * DH, PAIR * DH)
            part_ref[:, pl.ds(at, PAIR * DH)] = jnp.concatenate([acc[:text, :DH], acc[text:, :DH]], axis=1)
            lane = iota((text, LANES), 1)
            first = jnp.where(lane < 32, top[:text], acc[:text, DH:])
            second = jnp.where(lane < 96, top[text:], acc[text:, DH:])
            ml_ref[:, pl.ds(pl.multiple_of(u * LANES, LANES), LANES)] = jnp.where(lane < 64, first, second)

        over_pairs(score, weigh, (sa, sb))

    by_blocks(used, run)


def join_kernel(
    text_hbm, came_ref, part_ref, ml_ref, kvt, qx, bias_ref, counts_ref, out_hbm, text_ref, out_ref, sem_in, sem_out, qv, kt, vt, kv, vv, bias_v, va, ta, vb, tb
):
    text = text_hbm.shape[0]
    load = pltpu.make_async_copy(text_hbm.at[:, : GQ * DH], text_ref, sem_in)
    load.start()
    vis = came_ref.shape[0] // 2
    rows = text + vis
    q = GQ * DH
    a, b = iota((2 * vis, 2 * vis), 0), iota((2 * vis, 2 * vis), 1)
    src = ((a % vis) // CAP) * 8 + a % CAP + CAP * (a // vis)
    both = dot(ones_where(b == src).astype(BF16), came_ref[...])
    low, high = both[:vis], both[vis:]
    qv[...] = low[:, :q].astype(BF16)
    own_k = low[:, q:].astype(BF16)
    kv[:vis, :DH] = own_k
    kv[:vis, DH:] = jnp.zeros((vis, LANES), BF16)
    vv[:vis, :DH] = high[:, :DH].astype(BF16)
    vv[:, DH:] = jnp.ones((vv.shape[0], DH), BF16)
    pick0 = ones_where(iota((8, DH), 1) == 0).astype(BF16)
    own_live = dot_nt(pick0, own_k)[0:1] < DEAD / 2
    bias_v[:, :text] = bias_ref[:, :text]
    bias_v[:, text:] = jnp.where(own_live, bias_ref[:, text:], -BIG)
    live_q = jnp.broadcast_to(ones_where(low[:, q : q + 1] < DEAD / 2), (vis, LANES)) > 0.5
    used = jnp.sum(ones_where(counts_ref[:, :1] > 0.5)).astype(jnp.int32)
    lane = iota((vis, LANES), 1)
    place_r = (iota((vis, LANES), 0) + text).astype(F32)
    lane_t, place_t = iota((text, LANES), 1), iota((text, LANES), 0).astype(F32)
    kt[:, :DH] = kvt[:, :DH]
    kt[:text, DH:] = jnp.zeros((text, LANES), BF16)
    vt[:, :DH] = kvt[:, DH:]
    vt[:, DH:] = jnp.ones((vt.shape[0], DH), BF16)
    for k in range(1, REACH + 1):
        start = rows - counts_ref[k - 1 : k]
        lo = DH + 2 * DH * (k - 1)
        pk = high[:, lo : lo + DH]
        at = k * vis
        kv[at : at + vis, :DH] = pk.astype(BF16)
        vv[at : at + vis, :DH] = high[:, lo + DH : lo + 2 * DH].astype(BF16)
        live = jnp.broadcast_to(ones_where(pk[:, 0:1] < DEAD / 2), (vis, LANES)) > 0.5
        ok = (place_r >= start) & live
        kv[at : at + vis, DH:] = jnp.where(lane == 0, jnp.where(ok, 0.0, -BIG), ones_where(lane == 1)).astype(BF16)
        ok = jnp.where(place_t >= start, 0.0, -BIG)
        kt[k * text : (k + 1) * text, DH:] = jnp.where(lane_t == 0, ok, ones_where(lane_t == 1)).astype(BF16)

    load.wait()

    def run(blocks):
        split = blocks * text
        end = blocks * rows

        def score(u, bufs):
            ss, ts = bufs
            qe = pair_rows(qv, u, qx[text:])
            parts = []
            for k in range(blocks):
                s = dot_nt(qe, kt[k * text : (k + 1) * text])
                if k == 0:
                    s = s + twice(bias_v[:, :text])
                ss[:, k * text : (k + 1) * text] = s
                parts.append(s)
            s = dot_nt(qe, kv[:vis]) + twice(bias_v[:, text:])
            ss[:, split : split + vis] = s
            parts.append(s)
            if blocks > 1:
                s = dot_nt(qe, kv[vis : blocks * vis])
                ss[:, split + vis : end] = s
                parts.append(s)
            top_v = row_max(parts)
            ml = ml_ref[:, pl.ds(pl.multiple_of(u * LANES, LANES), LANES)]
            top_t = jnp.concatenate([ml[:, :1], ml[:, 64:65]], axis=0)
            if blocks > 1:
                s = dot_nt(pair_rows(text_ref, u, qx[:text]), kv[vis : blocks * vis])
                ts[:, : (blocks - 1) * vis] = s
                top_t = jnp.maximum(row_max([s]), top_t)
            return top_v, top_t

        def weigh(u, bufs, tops):
            ss, ts = bufs
            top_v, top_t = tops
            at = pl.multiple_of(u * PAIR * DH, PAIR * DH)
            p = jnp.exp2((ss[:, :end] - top_v) * SCALE).astype(BF16)
            acc = dot(p[:, :split], vt[:split]) + dot(p[:, split:], vv[: blocks * vis])
            out = acc[:, :DH] / acc[:, DH:]
            out = jnp.concatenate([jnp.where(live_q, out[:vis], 0.0), jnp.where(live_q, out[vis:], 0.0)], axis=1)
            out_ref[text:, pl.ds(at, PAIR * DH)] = out.astype(BF16)
            part = part_ref[:, pl.ds(at, PAIR * DH)]
            num = jnp.concatenate([part[:, :DH], part[:, DH:]], axis=0)
            ml = ml_ref[:, pl.ds(pl.multiple_of(u * LANES, LANES), LANES)]
            den = jnp.broadcast_to(jnp.concatenate([ml[:, 32:33], ml[:, 96:97]], axis=0), num.shape)
            if blocks > 1:
                p = jnp.exp2((ts[:, : (blocks - 1) * vis] - top_t) * SCALE).astype(BF16)
                was = jnp.concatenate([ml[:, :1], ml[:, 64:65]], axis=0)
                fade = jnp.broadcast_to(jnp.exp2((was - top_t) * SCALE), num.shape)
                acc = dot(p, vv[vis : blocks * vis])
                num = num * fade + acc[:, :DH]
                den = den * fade + acc[:, DH:]
            out = num / den
            out_ref[:text, pl.ds(at, PAIR * DH)] = jnp.concatenate([out[:text], out[text:]], axis=1).astype(BF16)
            place = pl.ds(at, PAIR * DH)
            pltpu.make_async_copy(out_ref.at[:, place], out_hbm.at[:, place], sem_out.at[u]).start()

        over_pairs(score, weigh, ((va, ta), (vb, tb)))
        for u in range(GQ // PAIR):
            place = pl.ds(u * PAIR * DH, PAIR * DH)
            pltpu.make_async_copy(out_ref.at[:, place], out_hbm.at[:, place], sem_out.at[u]).wait()

    by_blocks(used, run)


def cost(flops, nbytes):
    return pl.CostEstimate(flops=flops, bytes_accessed=nbytes, transcendentals=0)


def vmem(mib):
    return pltpu.CompilerParams(vmem_limit_bytes=mib << 20)


def layer(text_rows, vis_rows, vis_dest, segments):
    seq_count = lax.axis_size("seq")
    groups = lax.axis_size("group")
    text, _, wide = text_rows.shape
    per_dev, heads, _ = vis_rows.shape
    block = per_dev * heads
    vis = seq_count * CAP
    rows = text + vis
    q = GQ * DH
    total = groups * seq_count

    text2 = text_rows.reshape(text, wide)
    vis2 = vis_rows.reshape(block, wide)
    dest = vis_dest.reshape(1, per_dev)
    text_hbm = pltpu.with_memory_space_constraint(text2, pltpu.HBM)
    segs = segments.reshape(rows // LANES, LANES)
    tail_block = q // (2 * DH)
    step = pl.pallas_call(
        step_kernel,
        grid=(1,),
        in_specs=[
            pl.BlockSpec((block, 2 * DH), lambda i: (0, tail_block)),
            pl.BlockSpec((1, per_dev), lambda i: (0, 0)),
        ],
        out_specs=pl.BlockSpec((block + 8, 2 * DH), lambda i: (0, 0)),
        out_shape=jax.ShapeDtypeStruct((block + 8, 2 * DH), BF16),
        cost_estimate=cost(1000, 70_000),
        name="step_rows",
    )(vis2, dest)
    listed = pl.pallas_call(
        functools.partial(list_kernel, per_dev, heads),
        out_shape=jax.ShapeDtypeStruct((block, wide + LANES), BF16),
        cost_estimate=cost(15_000_000, 400_000),
        compiler_params=vmem(8),
        name="list_rows",
    )(vis2, dest)
    mine = pl.pallas_call(
        halo_kernel,
        grid=(1,),
        in_specs=[
            pl.BlockSpec((text, 2 * DH), lambda i: (0, tail_block)),
            pl.BlockSpec((rows // LANES, LANES), lambda i: (0, 0)),
        ],
        out_specs=pl.BlockSpec((text + 8, 2 * DH), lambda i: (0, 0)),
        out_shape=jax.ShapeDtypeStruct((text + 8, 2 * DH), BF16),
        cost_estimate=cost(1000, 300_000),
        name="halo_rows",
    )(text2, segs)
    step = lax.ppermute(step, "group", [(i, i + 1) for i in range(groups - 1)])

    far = lax.ppermute(mine, ("group", "seq"), [(o, o + REACH) for o in range(total - REACH)])
    near, seam = [], []
    for k in range(1, REACH):
        by = 1 if k == REACH - 1 else k
        pairs = [(s, s + by) for s in range(seq_count) if s % RING + by < RING]
        near.append(lax.ppermute(near[-1] if by < k else mine, "seq", pairs))
    for k in range(1, REACH):
        pairs = [(s + REACH - k, s) for s in range(seq_count) if s % RING < k]
        seam.append(lax.ppermute(far, "seq", pairs))

    listed = pl.pallas_call(
        functools.partial(add_kernel, per_dev, heads),
        out_shape=jax.ShapeDtypeStruct((block, wide + 2 * DH + 2 * LANES), BF16),
        cost_estimate=cost(2_000_000, 100_000),
        compiler_params=vmem(8),
        name="add_step",
    )(step, listed)
    own = lax.all_to_all(listed, "shard", split_axis=0, concat_axis=0, tiled=True)

    packed = pl.pallas_call(
        pack_kernel,
        out_shape=jax.ShapeDtypeStruct((seq_count * 8, DH + 2 * DH * REACH), BF16),
        cost_estimate=cost(200_000_000, 800_000),
        compiler_params=vmem(12),
        name="pack_rows",
    )(own)
    came = lax.all_to_all(packed, "seq", split_axis=0, concat_axis=0, tiled=True)

    keys = (REACH + 1) * text
    parts = pl.pallas_call(
        text_kernel,
        out_shape=[
            jax.ShapeDtypeStruct((text, q), F32),
            jax.ShapeDtypeStruct((text, q // PAIR), F32),
            jax.ShapeDtypeStruct((keys, 2 * DH), BF16),
            jax.ShapeDtypeStruct((rows, LANES), BF16),
            jax.ShapeDtypeStruct((vis, rows), F32),
            jax.ShapeDtypeStruct((8, LANES), F32),
        ],
        scratch_shapes=[
            pltpu.VMEM((keys, DH + LANES), BF16),
            pltpu.VMEM((keys, 2 * DH), BF16),
            pltpu.VMEM((text, text), F32),
            pltpu.VMEM((PAIR * text, keys), F32),
            pltpu.VMEM((PAIR * text, keys), F32),
        ],
        cost_estimate=cost(3_000_000_000, 4_000_000),
        compiler_params=vmem(20),
        name="attend_text",
    )(text_hbm, segs, *near, far, *seam)
    out = pl.pallas_call(
        join_kernel,
        out_shape=jax.ShapeDtypeStruct((rows, q), BF16),
        in_specs=[pl.BlockSpec(memory_space=pltpu.HBM)] + [pl.BlockSpec(memory_space=pltpu.VMEM)] * 7,
        out_specs=pl.BlockSpec(memory_space=pltpu.HBM),
        scratch_shapes=[
            pltpu.VMEM((text, q), BF16),
            pltpu.VMEM((rows, q), BF16),
            pltpu.SemaphoreType.DMA,
            pltpu.SemaphoreType.DMA((GQ // PAIR,)),
            pltpu.VMEM((vis, q), BF16),
            pltpu.VMEM((keys, DH + LANES), BF16),
            pltpu.VMEM((keys, 2 * DH), BF16),
            pltpu.VMEM(((REACH + 1) * vis, DH + LANES), BF16),
            pltpu.VMEM(((REACH + 1) * vis, 2 * DH), BF16),
            pltpu.VMEM((vis, rows), F32),
            pltpu.VMEM((PAIR * vis, (REACH + 1) * rows), F32),
            pltpu.VMEM((PAIR * text, REACH * vis), F32),
            pltpu.VMEM((PAIR * vis, (REACH + 1) * rows), F32),
            pltpu.VMEM((PAIR * text, REACH * vis), F32),
        ],
        cost_estimate=cost(3_000_000_000, 4_000_000),
        compiler_params=vmem(20),
        name="attend_join",
    )(text_hbm, came, *parts)
    return out.reshape(rows, 1, q)


def solution(mesh):
    placed = (
        P(("group", "seq"), "shard", None),
        P(("group", "seq", "shard"), None, None),
        P(("group", "seq", "shard"), None),
        P(("group", "seq")),
    )
    return jax.shard_map(
        layer,
        mesh=mesh,
        in_specs=placed,
        out_specs=P(("group", "seq"), "shard", None),
        check_vma=False,
    )
```
